512 devices in a mesh: row: 32 (over y, z_hi, x), col: 16 (over z_lo, core).
Axes of the slice: x: 4, y: 4, z: 16 (z_hi: 2, z_lo: 8; z = z_hi * 8 + z_lo), core: 2. Of those that a mesh axis runs over, the one named last changes fastest.
Arguments:
- query_field: bfloat16 [512, 256, 1152], P('row', 'col'), may hold values from -136 to 136
- key_field: bfloat16 [512, 256, 1152], P('row', 'col'), may hold values from -8.5 to 8.5
- value_field: bfloat16 [512, 256, 1152], P('row', 'col'), may hold values from -6 to 6
- query_tan: bfloat16 [512, 256, 1152], P('row', 'col'), may hold values from -6 to 6
- key_tan: bfloat16 [512, 256, 1152], P('row', 'col'), may hold values from -6 to 6
- value_tan: bfloat16 [512, 256, 1152], P('row', 'col'), may hold values from -6 to 6
- pool_near: float32 [4, 4], replicated, may hold values from -1.5 to 1.5
- pool_far: float32 [16, 16], replicated, may hold values from -0.375 to 0.375
- level_bias: float32 [2, 16], replicated, may hold values from 0.5 to 2.5
Outputs:
- mixed: bfloat16 [512, 256, 1152], P('row', 'col')
- mixed_tan: bfloat16 [512, 256, 1152], P('row', 'col')
The draws below stay inside these ranges and needn't reach their ends.
All inputs are finite; a program needn't handle non-finite values.
Results may differ from the reference program's by a relative error of at most 0.012.
Values may be sent and summed in bfloat16 or wider, within the bound.
A program may use at most 128 MiB of HBM per device.

```python
import jax
import jax.numpy as jnp
from jax import lax

D = 1152
HEADS = 16
HEAD_DIM = 72
WIN = 16
RIM = 8
NEAR_POOL = 4
GRID_ROWS = 512
GRID_COLS = 256
N_ROW = 32
N_COL = 16


def query_key_pair(key):
    grid_shape = (GRID_ROWS, GRID_COLS, D)
    queries = 1.4 * jax.random.truncated_normal(jax.random.fold_in(key, 101), -6.0, 6.0, grid_shape, jnp.float32)
    keyset = 1.4 * jax.random.truncated_normal(jax.random.fold_in(key, 102), -6.0, 6.0, grid_shape, jnp.float32)
    return (queries, keyset)


def draw_query_field(key, part):
    return query_key_pair(key)[0].astype(jnp.bfloat16)


def draw_key_field(key, part):
    return query_key_pair(key)[1].astype(jnp.bfloat16)


def level_of(key, extent, split, smallest, top_value):
    level = 1.0
    for position, parts in split:
        draws = jax.random.uniform(jax.random.fold_in(jax.random.fold_in(key, 6), position), (parts,), jnp.float32, smallest / len(split), top_value / len(split))
        level = level * jnp.repeat(jnp.exp(draws), extent[position] // parts).reshape((-1,) + (1,) * (len(extent) - 1 - position))
    return level


def normal_values(stream_key, extent, scale, reach, shards=(), held_as=jnp.bfloat16):
    result = scale * jax.random.normal(stream_key, extent, jnp.float32)
    if shards:
        result = result * level_of(stream_key, extent, shards, -0.22, 0.18)
    return jnp.clip(result, -reach, reach).astype(held_as)


def setup_inputs(seed: int = 0) -> dict:
    key_list = jax.random.split(jax.random.key(seed), 10)
    query_field = draw_query_field(jax.random.fold_in(key_list[9], 71), 0)
    key_field = draw_key_field(jax.random.fold_in(key_list[9], 71), 0)
    value_field = normal_values(key_list[2], (GRID_ROWS, GRID_COLS, D), 1.0, 6.0, ((0, 32), (1, 16)))
    query_tan = normal_values(key_list[3], (GRID_ROWS, GRID_COLS, D), 1.0, 6.0, ((0, 32), (1, 16)))
    key_tan = normal_values(key_list[4], (GRID_ROWS, GRID_COLS, D), 1.0, 6.0, ((0, 32), (1, 16)))
    value_tan = normal_values(key_list[5], (GRID_ROWS, GRID_COLS, D), 1.0, 6.0, ((0, 32), (1, 16)))
    pool_near = normal_values(key_list[6], (NEAR_POOL, NEAR_POOL), (NEAR_POOL * NEAR_POOL) ** -0.5, 1.5, (), jnp.float32)
    pool_far = normal_values(key_list[7], (WIN, WIN), (WIN * WIN) ** -0.5, 0.375, (), jnp.float32)
    level_bias = jnp.clip(jax.random.uniform(key_list[8], (2, HEADS), jnp.float32, 0.5, 2.5), 0.5, 2.5)
    return dict(query_field=query_field, key_field=key_field, value_field=value_field, query_tan=query_tan, key_tan=key_tan, value_tan=value_tan, pool_near=pool_near, pool_far=pool_far, level_bias=level_bias)


def pool_cells(field, weights, size):
    row_count, col_count, width = field.shape
    blocks = field.astype(jnp.float32).reshape(row_count // size, size, col_count // size, size, width)
    pooled = jnp.einsum('apbqd,pq->abd', blocks, weights, precision=lax.Precision.HIGHEST)
    return pooled.astype(jnp.bfloat16)


def attend(queries, queries_tan, key_sets, key_bias):
    count = queries.shape[0]
    score_scale = HEAD_DIM ** -0.5
    query_wide = queries.astype(jnp.float32).reshape(count, HEADS, HEAD_DIM)
    tan_wide = queries_tan.astype(jnp.float32).reshape(count, HEADS, HEAD_DIM)
    keys_wide = key_sets[0].astype(jnp.float32).reshape(-1, HEADS, HEAD_DIM)
    values_wide = key_sets[1].astype(jnp.float32).reshape(-1, HEADS, HEAD_DIM)
    keytan_wide = key_sets[2].astype(jnp.float32).reshape(-1, HEADS, HEAD_DIM)
    valtan_wide = key_sets[3].astype(jnp.float32).reshape(-1, HEADS, HEAD_DIM)
    scores = jnp.einsum('qhd,khd->hqk', query_wide, keys_wide) * score_scale + key_bias[:, None, :]
    tangent = (jnp.einsum('qhd,khd->hqk', tan_wide, keys_wide) + jnp.einsum('qhd,khd->hqk', query_wide, keytan_wide)) * score_scale
    top = jnp.max(scores, axis=-1, keepdims=True)
    expd = jnp.exp(scores - top)
    weights = expd / jnp.sum(expd, axis=-1, keepdims=True)
    weights_low = lax.optimization_barrier(weights.astype(jnp.bfloat16)).astype(jnp.float32)
    product = weights * tangent
    row_total = jnp.sum(product, axis=-1)
    product_low = lax.optimization_barrier(product.astype(jnp.bfloat16)).astype(jnp.float32)
    mix = jnp.einsum('hqk,khd->qhd', weights_low, values_wide)
    mix_tan = jnp.einsum('hqk,khd->qhd', product_low, values_wide) + jnp.einsum('hqk,khd->qhd', weights_low, valtan_wide) - jnp.transpose(row_total)[:, :, None] * mix
    return mix.reshape(count, D).astype(jnp.bfloat16), mix_tan.reshape(count, D).astype(jnp.bfloat16)


def reference(query_field, key_field, value_field, query_tan, key_tan, value_tan, pool_near, pool_far, level_bias):
    fields = (key_field, value_field, key_tan, value_tan)
    padded = jnp.stack([jnp.pad(one_field, ((RIM, RIM), (RIM, RIM), (0, 0))) for one_field in fields])
    near_grid = jnp.stack([pool_cells(one_field, pool_near, NEAR_POOL) for one_field in fields])
    far_keys = jnp.stack([pool_cells(one_field, pool_far, WIN).reshape(-1, D) for one_field in fields])
    span = WIN + 2 * RIM
    near_span = 2 * WIN // NEAR_POOL
    far_count = far_keys.shape[1]

    def one_tile(index):
        tile_row = index // N_COL
        tile_col = index % N_COL
        anchor = jnp.int32(0)
        fine = lax.dynamic_slice(padded, (anchor, tile_row * WIN, tile_col * WIN, anchor), (4, span, span, D)).reshape(4, span * span, D)
        near_block = lax.dynamic_slice(near_grid, (anchor, (tile_row // 2) * near_span, (tile_col // 2) * near_span, anchor), (4, near_span, near_span, D)).reshape(4, near_span * near_span, D)
        key_sets = jnp.concatenate([fine, near_block, far_keys], axis=1)
        row_ids = tile_row * WIN - RIM + jnp.arange(span, dtype=jnp.int32)
        col_ids = tile_col * WIN - RIM + jnp.arange(span, dtype=jnp.int32)
        row_ok = (row_ids >= 0) & (row_ids < GRID_ROWS)
        col_ok = (col_ids >= 0) & (col_ids < GRID_COLS)
        valid = (row_ok[:, None] & col_ok[None, :]).reshape(span * span)
        fine_bias = jnp.where(valid, jnp.float32(0.0), jnp.float32(-jnp.inf))
        key_bias = jnp.concatenate([
            jnp.broadcast_to(fine_bias[None, :], (HEADS, span * span)),
            jnp.broadcast_to(level_bias[0][:, None], (HEADS, near_span * near_span)),
            jnp.broadcast_to(level_bias[1][:, None], (HEADS, far_count))], axis=1)
        queries = lax.dynamic_slice(query_field, (tile_row * WIN, tile_col * WIN, anchor), (WIN, WIN, D)).reshape(WIN * WIN, D)
        queries_tan = lax.dynamic_slice(query_tan, (tile_row * WIN, tile_col * WIN, anchor), (WIN, WIN, D)).reshape(WIN * WIN, D)
        return attend(queries, queries_tan, key_sets, key_bias)

    mixed_tiles, tan_tiles = lax.map(one_tile, jnp.arange(N_ROW * N_COL, dtype=jnp.int32))

    def assemble(tiles):
        return tiles.reshape(N_ROW, N_COL, WIN, WIN, D).transpose(0, 2, 1, 3, 4).reshape(GRID_ROWS, GRID_COLS, D)

    return assemble(mixed_tiles), assemble(tan_tiles)
```

```python
import functools
import math

import jax
import jax.numpy as jnp
import numpy as np
from jax import lax
from jax.experimental import pallas as pl
from jax.experimental.pallas import tpu as pltpu
from jax.sharding import PartitionSpec as P

HEADS = 16
HEAD_DIM = 72
D = 1152
WIN = 16
CELLS = WIN * WIN
NX, NY, NZ = 4, 4, 16
LANES = 384
CHUNKS = D // LANES
MESH = pl.DeviceIdType.MESH
LOG2E = math.log2(math.e)
SCALE = HEAD_DIM**-0.5
NEG = -1e30

OWN, TOP, BOTTOM, LEFT, RIGHT = 0, 32, 48, 64, 80
TL, TR, BL, BR = 96, 104, 112, 120
NEAR, FAR, PAD = 128, 136, 200
GROUPS = 208
KEYS = GROUPS * 8
BLOCK = 32


def prep_kernel(w_ref, k_ref, v_ref, kt_ref, vt_ref, stack_ref, near_ref, far_ref):
    w = w_ref[...]
    hi = w.astype(jnp.bfloat16)
    rest = w - hi.astype(jnp.float32)
    mid = rest.astype(jnp.bfloat16)
    low = (rest - mid.astype(jnp.float32)).astype(jnp.bfloat16)
    far_rows = []
    for f, ref in enumerate((k_ref, v_ref, kt_ref, vt_ref)):
        cells = ref[...]
        stack_ref[f] = cells
        flat = cells.reshape(CELLS, D)
        pooled = jnp.dot(low, flat, preferred_element_type=jnp.float32)
        pooled += jnp.dot(mid, flat, preferred_element_type=jnp.float32)
        pooled += jnp.dot(hi, flat, preferred_element_type=jnp.float32)
        near_ref[f] = pooled[:16].astype(jnp.bfloat16)
        far_rows.append(pooled[16:17])
    far_ref[...] = jnp.concatenate(far_rows, axis=0).astype(jnp.bfloat16)


def place():
    r, c = lax.axis_index("row"), lax.axis_index("col")
    y, x = r // 8, lax.rem(r, 4)
    z = lax.rem(r // 4, 2) * 8 + c // 2
    return r, c, x, y, z, lax.rem(c, 2)


def device(x, y, z, core):
    return (y * 8 + (z // 8) * 4 + x, lax.rem(z, 8) * 2 + core)


def main_kernel(
    stack, near_in, far_in, q_in, qt_in, bias_ref,
    mix_ref, tan_ref,
    keys, zbuf, q_ref, qt_ref, s_ref, t_ref, w_ref, mix_acc, tan_acc,
    halo_send, halo_recv, misc_send, misc_recv, local_sem,
):
    r, c, x, y, z, core = place()
    up, down, west, east = r > 0, r < 31, c > 0, c < 15
    z_peers = [lax.rem(z + k, NZ) for k in range(1, NZ)]
    x_peers = [lax.rem(x + k, NX) for k in range(1, NX)]
    y_peers = [lax.rem(y + k, NY) for k in range(1, NY)]
    x_near = x + 1 - 2 * lax.rem(x, 2)
    near_peers = [device(x_near, y, z, core), device(x, y, z, 1 - core), device(x_near, y, z, 1 - core)]

    def lanes(chunk):
        return pl.ds(pl.multiple_of(chunk * LANES, 128), LANES)

    def part(first, count, chunk=None):
        width = slice(None) if chunk is None else lanes(chunk)
        return keys.at[:, pl.ds(first, count), :, width]

    def strips(chunk):
        out = []
        for half in range(2):
            out.append((down, stack.at[:, pl.ds(8, 8), half, :, lanes(chunk)], TOP + 8 * half, 8, (r + 1, c), up))
            out.append((up, stack.at[:, pl.ds(0, 8), half, :, lanes(chunk)], BOTTOM + 8 * half, 8, (r - 1, c), down))
        return out

    def sides(chunk):
        return [
            (east, stack.at[:, :, 1, :, lanes(chunk)], LEFT, 16, (r, c + 1), west),
            (west, stack.at[:, :, 0, :, lanes(chunk)], RIGHT, 16, (r, c - 1), east),
        ]

    def corners(chunk):
        return [
            (up & east, part(TOP + 8, 8, chunk), TL, 8, (r, c + 1), up & west),
            (up & west, part(TOP, 8, chunk), TR, 8, (r, c - 1), up & east),
            (down & east, part(BOTTOM + 8, 8, chunk), BL, 8, (r, c + 1), down & west),
            (down & west, part(BOTTOM, 8, chunk), BR, 8, (r, c - 1), down & east),
        ]

    def run(make, base, chunk, what):
        for n, (sends, src, first, count, target, receives) in enumerate(make(chunk)):
            slot = chunk * 10 + base + n
            copy = pltpu.make_async_remote_copy(
                src_ref=src, dst_ref=part(first, count, chunk),
                send_sem=halo_send.at[slot], recv_sem=halo_recv.at[slot],
                device_id=target, device_id_type=MESH,
            )
            if what == "start":
                pl.when(sends)(copy.start)
            elif what == "recv":
                pl.when(receives)(copy.wait_recv)
            else:
                pl.when(sends)(copy.wait_send)

    def to(src, dst, slot, target):
        return pltpu.make_async_remote_copy(
            src_ref=src, dst_ref=dst, send_sem=misc_send.at[slot], recv_sem=misc_recv.at[slot],
            device_id=target, device_id_type=MESH,
        )

    def drained(ref, sem):
        pltpu.make_async_copy(ref, ref, sem).wait()

    local = [
        pltpu.make_async_copy(stack.at[:, :, half], keys.at[:, pl.ds(OWN + 16 * half, 16)], local_sem.at[half])
        for half in range(2)
    ]
    near_slot = NEAR + 2 * (lax.rem(x, 2) * 2 + core)
    local.append(pltpu.make_async_copy(near_in, part(near_slot, 2), local_sem.at[2]))
    local.append(pltpu.make_async_copy(q_in, q_ref, local_sem.at[3]))
    local.append(pltpu.make_async_copy(qt_in, qt_ref, local_sem.at[4]))
    for copy in local:
        copy.start()

    barrier = pltpu.get_barrier_semaphore()

    def greet(target):
        pl.semaphore_signal(barrier, inc=1, device_id=target, device_id_type=MESH)

    for cond, target in ((down, (r + 1, c)), (up, (r - 1, c)), (east, (r, c + 1)), (west, (r, c - 1))):
        pl.when(cond)(functools.partial(greet, target))
    fixed = (
        [device(x, y, p, core) for p in z_peers]
        + [device(p, y, z, core) for p in x_peers]
        + [device(x, p, z, core) for p in y_peers]
        + [device(x, y, z, 1 - core), device(x_near, y, z, 1 - core)]
    )
    for target in fixed:
        greet(target)
    edges = sum(cond.astype(jnp.int32) for cond in (down, up, east, west))
    pl.semaphore_wait(barrier, len(fixed) + edges)

    for p in z_peers:
        to(far_in, zbuf.at[z], 0, device(x, y, p, core)).start()
    own_far = pltpu.make_async_copy(far_in, zbuf.at[z], local_sem.at[5])
    own_far.start()
    for target in near_peers:
        to(near_in, part(near_slot, 2), 4, target).start()
    for chunk in range(CHUNKS):
        run(strips, 0, chunk, "start")
        run(sides, 4, chunk, "start")

    def clear(first, count):
        keys[:, pl.ds(first, count)] = jnp.zeros((4, count, 8, D), jnp.bfloat16)

    clear(PAD, GROUPS - PAD)
    for present, first, count in ((up, TOP, 16), (down, BOTTOM, 16), (west, LEFT, 16), (east, RIGHT, 16)):
        pl.when(jnp.logical_not(present))(functools.partial(clear, first, count))
    for present, first in ((up & west, TL), (up & east, TR), (down & west, BL), (down & east, BR)):
        pl.when(jnp.logical_not(present))(functools.partial(clear, first, 8))

    far_group = FAR + 32 * core + 8 * y + 2 * x
    own_far.wait()
    drained(zbuf.at[pl.ds(0, NZ - 1)], misc_recv.at[0])
    for f in range(4):
        cells = jnp.concatenate([zbuf[n].astype(jnp.float32)[f : f + 1] for n in range(NZ)], axis=0)
        keys[f, pl.ds(far_group, 2)] = cells.astype(jnp.bfloat16).reshape(2, 8, D)
    for copy in local:
        copy.wait()
    for p in x_peers:
        to(part(far_group, 2), part(far_group, 2), 1, device(p, y, z, core)).start()
    drained(part(FAR, 6), misc_recv.at[1])
    far_y = FAR + 32 * core + 8 * y
    for p in y_peers:
        to(part(far_y, 8), part(far_y, 8), 2, device(x, p, z, core)).start()
    run(strips, 0, 0, "recv")
    run(corners, 6, 0, "start")
    drained(part(FAR, 24), misc_recv.at[2])
    far_core = FAR + 32 * core
    swap = to(part(far_core, 32), part(far_core, 32), 3, device(x, y, z, 1 - core))
    swap.start()
    drained(part(NEAR, 6), misc_recv.at[4])

    def load(f, tile, count):
        width = 128 * count
        return keys[f, :, :, pl.ds(pl.multiple_of(tile * 128, 128), width)].reshape(KEYS, width)

    def query(ref, tile, count):
        width = 128 * count
        return ref[:, :, pl.ds(pl.multiple_of(tile * 128, 128), width)].reshape(CELLS, width)

    def in_head(head, tile, count):
        lane = lax.broadcasted_iota(jnp.int32, (1, 128 * count), 1) + tile * 128 - head * HEAD_DIM
        return (lane >= 0) & (lane < HEAD_DIM)

    def nt(a, b):
        return lax.dot_general(a, b, (((1,), (1,)), ((), ())), preferred_element_type=jnp.float32)

    def nn(a, b):
        return jnp.dot(a, b, preferred_element_type=jnp.float32)

    def softmax(head):
        bias = bias_ref[head]

        def block(n, carry):
            rows = pl.ds(pl.multiple_of(n * BLOCK, BLOCK), BLOCK)
            top = None
            for tile in range(KEYS // 128):
                cols = slice(tile * 128, tile * 128 + 128)
                scores = s_ref[rows, cols] * (SCALE * LOG2E) + bias[:, cols]
                s_ref[rows, cols] = scores
                top = scores if top is None else jnp.maximum(top, scores)
            top = jnp.max(top, axis=1, keepdims=True)
            total = None
            for tile in range(KEYS // 128):
                cols = slice(tile * 128, tile * 128 + 128)
                expd = jnp.exp2(s_ref[rows, cols] - top)
                s_ref[rows, cols] = expd
                total = expd if total is None else total + expd
            inverse = 1.0 / jnp.sum(total, axis=1, keepdims=True)
            late = pl.ds(pl.multiple_of(CELLS + n * BLOCK, BLOCK), BLOCK)
            row_total = None
            for tile in range(KEYS // 128):
                cols = slice(tile * 128, tile * 128 + 128)
                weights = s_ref[rows, cols] * inverse
                product = weights * (t_ref[rows, cols] * SCALE)
                w_ref[rows, cols] = weights.astype(jnp.bfloat16)
                w_ref[late, cols] = product.astype(jnp.bfloat16)
                row_total = product if row_total is None else row_total + product
            row_sum = jnp.sum(row_total, axis=1, keepdims=True)
            t_ref[rows, 0:128] = jnp.broadcast_to(row_sum, (BLOCK, 128))
            return carry

        lax.fori_loop(0, CELLS // BLOCK, block, 0)

    def finish(head, tile, count, mix, product_mix, weight_tan):
        cols = pl.ds(pl.multiple_of(tile * 128, 128), 128 * count)
        keep = in_head(head, tile, count)
        row_total = t_ref[:, 0:128]
        if count == 2:
            row_total = jnp.concatenate([row_total, row_total], axis=1)
        mix_tan = product_mix + weight_tan - row_total * mix
        mix_acc[:, cols] = jnp.where(keep, mix, mix_acc[:, cols])
        tan_acc[:, cols] = jnp.where(keep, mix_tan, tan_acc[:, cols])

    def step(n, carry):
        late = (n >= 4).astype(jnp.int32)
        head, tile = 2 * n + late, n + late
        mask = in_head(head, tile, 1).astype(jnp.float32).astype(jnp.bfloat16)
        q = query(q_ref, tile, 1) * mask
        qt = query(qt_ref, tile, 1) * mask
        both = jnp.concatenate([jnp.concatenate([q, jnp.zeros_like(q)], 1), jnp.concatenate([qt, q], 1)], 0)
        scores = nt(both, jnp.concatenate([load(0, tile, 1), load(2, tile, 1)], 1))
        s_ref[...] = scores[:CELLS]
        t_ref[...] = scores[CELLS:]
        softmax(head)
        mixed = nn(w_ref[...], jnp.concatenate([load(1, tile, 1), load(3, tile, 1)], 1))
        finish(head, tile, 1, mixed[:CELLS, :128], mixed[CELLS:, :128], mixed[:CELLS, 128:])
        head, tile = 2 * n + 1 - late, n
        mask = in_head(head, tile, 2).astype(jnp.float32).astype(jnp.bfloat16)
        q = query(q_ref, tile, 2) * mask
        qt = query(qt_ref, tile, 2) * mask
        scores = nt(jnp.concatenate([q, qt], 0), load(0, tile, 2))
        s_ref[...] = scores[:CELLS]
        t_ref[...] = scores[CELLS:] + nt(q, load(2, tile, 2))
        softmax(head)
        mixed = nn(w_ref[...], load(1, tile, 2))
        finish(head, tile, 2, mixed[:CELLS], mixed[CELLS:], nn(w_ref[pl.ds(0, CELLS), :], load(3, tile, 2)))
        return carry

    def chunk_step(chunk, carry):
        @pl.when(chunk > 0)
        def _():
            run(strips, 0, chunk, "recv")
            run(corners, 6, chunk, "start")

        @pl.when(chunk == 0)
        def _():
            swap.wait_recv()

        run(sides, 4, chunk, "recv")
        run(corners, 6, chunk, "recv")
        lax.fori_loop(jnp.maximum(3 * chunk - 1, 0), 3 * chunk + 2, step, 0)
        return carry

    lax.fori_loop(0, CHUNKS, chunk_step, 0)
    mix_ref[...] = mix_acc[...].astype(jnp.bfloat16).reshape(WIN, WIN, D)
    tan_ref[...] = tan_acc[...].astype(jnp.bfloat16).reshape(WIN, WIN, D)

    for chunk in range(CHUNKS):
        run(strips, 0, chunk, "sent")
        run(sides, 4, chunk, "sent")
        run(corners, 6, chunk, "sent")
    drained(zbuf.at[pl.ds(0, NZ - 1)], misc_send.at[0])
    drained(part(FAR, 6), misc_send.at[1])
    drained(part(FAR, 24), misc_send.at[2])
    swap.wait_send()
    drained(part(NEAR, 6), misc_send.at[4])


def pool_weights(pool_near, pool_far):
    cell = np.arange(CELLS)
    block = (cell // 64) * 4 + (cell % 16) // 4
    member = jnp.asarray(np.arange(16)[:, None] == block[None, :])
    near = jnp.where(member, jnp.tile(pool_near, (4, 4)).reshape(1, CELLS), 0.0)
    return jnp.concatenate([near, pool_far.reshape(1, CELLS), jnp.zeros((7, CELLS), jnp.float32)], axis=0)


def key_bias(level_bias):
    r, c = lax.axis_index("row"), lax.axis_index("col")
    group = np.arange(GROUPS)

    def within(first, count):
        return (group >= first) & (group < first + count)

    top = within(TOP, 16) | within(TL, 8) | within(TR, 8)
    bottom = within(BOTTOM, 16) | within(BL, 8) | within(BR, 8)
    left = within(LEFT, 16) | within(TL, 8) | within(BL, 8)
    right = within(RIGHT, 16) | within(TR, 8) | within(BR, 8)
    gone = (r == 0) & top | (r == 31) & bottom | (c == 0) & left | (c == 15) & right
    gone = gone | (group >= PAD)
    bias = jnp.where(within(NEAR, 8), level_bias[0][:, None], jnp.where(within(FAR, 64), level_bias[1][:, None], 0.0))
    bias = jnp.where(gone[None, :], NEG, bias * LOG2E)
    return jnp.repeat(bias, 8, axis=1).reshape(HEADS, 1, KEYS)


def body(query_field, key_field, value_field, query_tan, key_tan, value_tan, pool_near, pool_far, level_bias):
    vmem = pl.BlockSpec(memory_space=pltpu.VMEM)
    anywhere = pl.BlockSpec(memory_space=pl.ANY)
    field = jax.ShapeDtypeStruct((WIN, WIN, D), jnp.bfloat16)
    stack, near, far = pl.pallas_call(
        prep_kernel,
        out_shape=(
            jax.ShapeDtypeStruct((4, WIN, WIN, D), jnp.bfloat16),
            jax.ShapeDtypeStruct((4, 16, D), jnp.bfloat16),
            jax.ShapeDtypeStruct((4, D), jnp.bfloat16),
        ),
        in_specs=[vmem] * 5,
        out_specs=(vmem, vmem, vmem),
        name="prep",
    )(pool_weights(pool_near, pool_far), key_field, value_field, key_tan, value_tan)
    halo = 10 * CHUNKS
    return pl.pallas_call(
        main_kernel,
        out_shape=(field, field),
        in_specs=[anywhere] * 5 + [vmem],
        out_specs=(vmem, vmem),
        scratch_shapes=[
            pltpu.VMEM((4, GROUPS, 8, D), jnp.bfloat16),
            pltpu.VMEM((NZ, 4, D), jnp.bfloat16),
            pltpu.VMEM((WIN, WIN, D), jnp.bfloat16),
            pltpu.VMEM((WIN, WIN, D), jnp.bfloat16),
            pltpu.VMEM((CELLS, KEYS), jnp.float32),
            pltpu.VMEM((CELLS, KEYS), jnp.float32),
            pltpu.VMEM((2 * CELLS, KEYS), jnp.bfloat16),
            pltpu.VMEM((CELLS, D), jnp.float32),
            pltpu.VMEM((CELLS, D), jnp.float32),
            pltpu.SemaphoreType.DMA((halo,)),
            pltpu.SemaphoreType.DMA((halo,)),
            pltpu.SemaphoreType.DMA((5,)),
            pltpu.SemaphoreType.DMA((5,)),
            pltpu.SemaphoreType.DMA((6,)),
        ],
        compiler_params=pltpu.CompilerParams(
            collective_id=0, has_side_effects=True, vmem_limit_bytes=60 * 1024 * 1024
        ),
        name="focal",
    )(
        stack.reshape(4, WIN, 2, 8, D), near.reshape(4, 2, 8, D), far, query_field, query_tan, key_bias(level_bias)
    )


def solution(mesh):
    spec = P("row", "col", None)
    return jax.shard_map(
        body, mesh=mesh, in_specs=(spec,) * 6 + (P(),) * 3, out_specs=(spec, spec), check_vma=False
    )
```

```python
import functools
import math

import jax
import jax.numpy as jnp
import numpy as np
from jax import lax
from jax.experimental import pallas as pl
from jax.experimental.pallas import tpu as pltpu
from jax.sharding import PartitionSpec as P

HEADS = 16
HEAD_DIM = 72
D = 1152
WIN = 16
CELLS = WIN * WIN
NX, NY, NZ = 4, 4, 16
EDGES = (0, 384, 640, 896, 1152)
CHUNKS = len(EDGES) - 1
MESH = pl.DeviceIdType.MESH
LOG2E = math.log2(math.e)
SCALE = HEAD_DIM**-0.5
NEG = -1e30

OWN, TOP, BOTTOM, LEFT, RIGHT = 0, 32, 48, 64, 80
TL, TR, BL, BR = 96, 104, 112, 120
NEAR, PAD, FAR = 128, 136, 144
GROUPS = 208
KEYS = GROUPS * 8
BLOCK = 32


def prep_kernel(w_ref, k_ref, v_ref, kt_ref, vt_ref, stack_ref, near_ref, far_ref):
    w = w_ref[...]
    hi = w.astype(jnp.bfloat16)
    rest = w - hi.astype(jnp.float32)
    mid = rest.astype(jnp.bfloat16)
    low = (rest - mid.astype(jnp.float32)).astype(jnp.bfloat16)
    far_rows = []
    for f, ref in enumerate((k_ref, v_ref, kt_ref, vt_ref)):
        cells = ref[...]
        stack_ref[f] = cells
        flat = cells.reshape(CELLS, D)
        pooled = jnp.dot(low, flat, preferred_element_type=jnp.float32)
        pooled += jnp.dot(mid, flat, preferred_element_type=jnp.float32)
        pooled += jnp.dot(hi, flat, preferred_element_type=jnp.float32)
        near_ref[f] = pooled[:16].astype(jnp.bfloat16)
        far_rows.append(pooled[16:17])
    far_ref[...] = jnp.concatenate(far_rows, axis=0).astype(jnp.bfloat16)


def place():
    r, c = lax.axis_index("row"), lax.axis_index("col")
    y, x = r // 8, lax.rem(r, 4)
    z = lax.rem(r // 4, 2) * 8 + c // 2
    return r, c, x, y, z, lax.rem(c, 2)


def device(x, y, z, core):
    return (y * 8 + (z // 8) * 4 + x, lax.rem(z, 8) * 2 + core)


def main_kernel(
    stack, near_in, far_in, q_in, qt_in, bias_ref,
    mix_ref, tan_ref,
    keys, zbuf, relay, q_ref, qt_ref, s_ref, t_ref, w_ref, mix_acc, tan_acc,
    halo_send, halo_recv, relay_send, relay_recv, misc_send, misc_recv, local_sem,
):
    r, c, x, y, z, core = place()
    up, down, west, east = r > 0, r < 31, c > 0, c < 15
    z_peers = [lax.rem(z + k, NZ) for k in range(1, NZ)]
    x_peers = [lax.rem(x + k, NX) for k in range(1, NX)]
    y_peers = [lax.rem(y + k, NY) for k in range(1, NY)]
    x_near = x + 1 - 2 * lax.rem(x, 2)
    near_peers = [device(x_near, y, z, core), device(x, y, z, 1 - core), device(x_near, y, z, 1 - core)]

    def lanes(chunk, last=None):
        last = chunk if last is None else last
        return pl.ds(EDGES[chunk], EDGES[last + 1] - EDGES[chunk])

    def part(first, count, chunk=None, last=None):
        width = slice(None) if chunk is None else lanes(chunk, last)
        return keys.at[:, pl.ds(first, count), :, width]

    place_x = lax.rem(r, 4)
    far_down, far_up = down & (place_x == 3), up & (place_x == 0)
    hops = jnp.where(place_x >= 2, 2, -2)
    paired = (r + hops >= 0) & (r + hops < 32)
    relays_down, relays_up = paired & (place_x == 2), paired & (place_x == 1)

    def strips(chunk):
        low = [stack.at[:, pl.ds(8, 8), half, :, lanes(chunk)] for half in range(2)]
        high = [stack.at[:, pl.ds(0, 8), half, :, lanes(chunk)] for half in range(2)]
        return [
            (down, low[0], TOP, 8, (r + 1, c), up),
            (up, high[0], BOTTOM, 8, (r - 1, c), down),
            (down & (place_x != 3), low[1], TOP + 8, 8, (r + 1, c), up),
            (up & (place_x != 0), high[1], BOTTOM + 8, 8, (r - 1, c), down),
        ]

    def relay_in(chunk, what):
        for n, cond, row, target in ((2, far_down, 8, (r - 1, c)), (3, far_up, 0, (r + 1, c))):
            copy = pltpu.make_async_remote_copy(
                src_ref=stack.at[:, pl.ds(row, 8), 1, :, lanes(chunk)], dst_ref=relay.at[:, :, :, lanes(chunk)],
                send_sem=halo_send.at[chunk * 10 + n], recv_sem=relay_recv.at[chunk],
                device_id=target, device_id_type=MESH,
            )
            pl.when(cond)(copy.start if what == "start" else copy.wait_send)

    def relay_out(chunk, what):
        for n, cond, first, row in ((2, relays_down, TOP + 8, r + 2), (3, relays_up, BOTTOM + 8, r - 2)):
            copy = pltpu.make_async_remote_copy(
                src_ref=relay.at[:, :, :, lanes(chunk)], dst_ref=part(first, 8, chunk),
                send_sem=relay_send.at[chunk], recv_sem=halo_recv.at[chunk * 10 + n],
                device_id=(row, c), device_id_type=MESH,
            )
            if what == "start":
                arrived = relay.at[:, :, :, lanes(chunk)]

                @pl.when(cond)
                def _(copy=copy, arrived=arrived):
                    drained(arrived, relay_recv.at[chunk])
                    copy.start()
            else:
                pl.when(cond)(copy.wait_send)

    def sides(chunk):
        return [
            (east, stack.at[:, :, 1, :, lanes(chunk)], LEFT, 16, (r, c + 1), west),
            (west, stack.at[:, :, 0, :, lanes(chunk)], RIGHT, 16, (r, c - 1), east),
        ]

    def corners(chunk):
        return [
            (up & east, part(TOP + 8, 8, chunk), TL, 8, (r, c + 1), up & west),
            (up & west, part(TOP, 8, chunk), TR, 8, (r, c - 1), up & east),
            (down & east, part(BOTTOM + 8, 8, chunk), BL, 8, (r, c + 1), down & west),
            (down & west, part(BOTTOM, 8, chunk), BR, 8, (r, c - 1), down & east),
        ]

    def run(make, base, chunk, what):
        for n, (sends, src, first, count, target, receives) in enumerate(make(chunk)):
            slot = chunk * 10 + base + n
            copy = pltpu.make_async_remote_copy(
                src_ref=src, dst_ref=part(first, count, chunk),
                send_sem=halo_send.at[slot], recv_sem=halo_recv.at[slot],
                device_id=target, device_id_type=MESH,
            )
            if what == "start":
                pl.when(sends)(copy.start)
            elif what == "recv":
                pl.when(receives)(copy.wait_recv)
            else:
                pl.when(sends)(copy.wait_send)

    def to(src, dst, slot, target):
        return pltpu.make_async_remote_copy(
            src_ref=src, dst_ref=dst, send_sem=misc_send.at[slot], recv_sem=misc_recv.at[slot],
            device_id=target, device_id_type=MESH,
        )

    def drained(ref, sem):
        pltpu.make_async_copy(ref, ref, sem).wait()

    local = [
        pltpu.make_async_copy(stack.at[:, :, half], keys.at[:, pl.ds(OWN + 16 * half, 16)], local_sem.at[half])
        for half in range(2)
    ]
    near_slot = NEAR + 2 * (lax.rem(x, 2) * 2 + core)
    local.append(pltpu.make_async_copy(near_in, part(near_slot, 2), local_sem.at[2]))
    local.append(pltpu.make_async_copy(q_in, q_ref, local_sem.at[3]))
    local.append(pltpu.make_async_copy(qt_in, qt_ref, local_sem.at[4]))
    for copy in local:
        copy.start()

    barrier = pltpu.get_barrier_semaphore()

    def greet(target):
        pl.semaphore_signal(barrier, inc=1, device_id=target, device_id_type=MESH)

    for cond, target in ((down, (r + 1, c)), (up, (r - 1, c)), (east, (r, c + 1)), (west, (r, c - 1))):
        pl.when(cond)(functools.partial(greet, target))
    fixed = (
        [device(x, y, p, core) for p in z_peers]
        + [device(p, y, z, core) for p in x_peers]
        + [device(x, p, z, core) for p in y_peers]
        + [device(x, y, z, 1 - core), device(x_near, y, z, 1 - core)]
    )
    for target in fixed:
        greet(target)
    pl.when(paired)(functools.partial(greet, (r + hops, c)))
    edges = sum(cond.astype(jnp.int32) for cond in (down, up, east, west, paired))
    pl.semaphore_wait(barrier, len(fixed) + edges)

    relay_in(0, "start")
    for p in z_peers:
        to(far_in, zbuf.at[z], 0, device(x, y, p, core)).start()
    own_far = pltpu.make_async_copy(far_in, zbuf.at[z], local_sem.at[5])
    own_far.start()
    run(strips, 0, 0, "start")
    run(sides, 4, 0, "start")
    for target in near_peers:
        to(near_in, part(near_slot, 2), 4, target).start()

    def clear(first, count):
        keys[:, pl.ds(first, count)] = jnp.zeros((4, count, 8, D), jnp.bfloat16)

    clear(PAD, FAR - PAD)
    for present, first, count in ((up, TOP, 16), (down, BOTTOM, 16), (west, LEFT, 16), (east, RIGHT, 16)):
        pl.when(jnp.logical_not(present))(functools.partial(clear, first, count))
    for present, first in ((up & west, TL), (up & east, TR), (down & west, BL), (down & east, BR)):
        pl.when(jnp.logical_not(present))(functools.partial(clear, first, 8))

    relay_out(0, "start")
    far_group = FAR + 32 * core + 8 * y + 2 * x
    own_far.wait()
    drained(zbuf.at[pl.ds(0, NZ - 1)], misc_recv.at[0])
    for f in range(4):
        cells = jnp.concatenate([zbuf[n].astype(jnp.float32)[f : f + 1] for n in range(NZ)], axis=0)
        keys[f, pl.ds(far_group, 2)] = cells.astype(jnp.bfloat16).reshape(2, 8, D)
    for copy in local:
        copy.wait()
    for p in x_peers:
        to(part(far_group, 2), part(far_group, 2), 1, device(p, y, z, core)).start()
    for chunk in range(1, CHUNKS):
        relay_in(chunk, "start")
    drained(part(FAR, 6), misc_recv.at[1])
    far_y, far_core = FAR + 32 * core + 8 * y, FAR + 32 * core
    groups = ((0, 0), (1, CHUNKS - 1))

    def send_y(n):
        for p in y_peers:
            to(part(far_y, 8, *groups[n]), part(far_y, 8, *groups[n]), 2 + n, device(x, p, z, core)).start()

    swaps = [
        to(part(far_core, 32, *span), part(far_core, 32, *span), 5 + n, device(x, y, z, 1 - core))
        for n, span in enumerate(groups)
    ]
    send_y(0)
    drained(part(FAR, 24, *groups[0]), misc_recv.at[2])
    swaps[0].start()
    send_y(1)

    def advance(chunk):
        run(strips, 0, chunk, "recv")
        run(corners, 6, chunk, "start")
        if chunk + 1 < CHUNKS:
            run(strips, 0, chunk + 1, "start")
            run(sides, 4, chunk + 1, "start")
            relay_out(chunk + 1, "start")

    advance(0)
    drained(part(FAR, 24, *groups[1]), misc_recv.at[3])
    swaps[1].start()
    drained(part(NEAR, 6), misc_recv.at[4])

    def load(f, tile, count):
        width = 128 * count
        return keys[f, :, :, pl.ds(pl.multiple_of(tile * 128, 128), width)].reshape(KEYS, width)

    def query(ref, tile, count):
        width = 128 * count
        return ref[:, :, pl.ds(pl.multiple_of(tile * 128, 128), width)].reshape(CELLS, width)

    def in_head(head, tile, count):
        lane = lax.broadcasted_iota(jnp.int32, (1, 128 * count), 1) + tile * 128 - head * HEAD_DIM
        return (lane >= 0) & (lane < HEAD_DIM)

    def nt(a, b):
        return lax.dot_general(a, b, (((1,), (1,)), ((), ())), preferred_element_type=jnp.float32)

    def nn(a, b):
        return jnp.dot(a, b, preferred_element_type=jnp.float32)

    def softmax(head):
        bias = bias_ref[head]

        def block(n, carry):
            rows = pl.ds(pl.multiple_of(n * BLOCK, BLOCK), BLOCK)
            top = None
            for tile in range(KEYS // 128):
                cols = slice(tile * 128, tile * 128 + 128)
                scores = s_ref[rows, cols] * (SCALE * LOG2E) + bias[:, cols]
                s_ref[rows, cols] = scores
                top = scores if top is None else jnp.maximum(top, scores)
            top = jnp.max(top, axis=1, keepdims=True)
            total = None
            for tile in range(KEYS // 128):
                cols = slice(tile * 128, tile * 128 + 128)
                expd = jnp.exp2(s_ref[rows, cols] - top)
                s_ref[rows, cols] = expd
                total = expd if total is None else total + expd
            inverse = 1.0 / jnp.sum(total, axis=1, keepdims=True)
            late = pl.ds(pl.multiple_of(CELLS + n * BLOCK, BLOCK), BLOCK)
            row_total = None
            for tile in range(KEYS // 128):
                cols = slice(tile * 128, tile * 128 + 128)
                weights = s_ref[rows, cols] * inverse
                product = weights * (t_ref[rows, cols] * SCALE)
                w_ref[rows, cols] = weights.astype(jnp.bfloat16)
                w_ref[late, cols] = product.astype(jnp.bfloat16)
                row_total = product if row_total is None else row_total + product
            row_sum = jnp.sum(row_total, axis=1, keepdims=True)
            t_ref[rows, 0:128] = jnp.broadcast_to(row_sum, (BLOCK, 128))
            return carry

        lax.fori_loop(0, CELLS // BLOCK, block, 0)

    def finish(head, tile, count, mix, product_mix, weight_tan):
        cols = pl.ds(pl.multiple_of(tile * 128, 128), 128 * count)
        keep = in_head(head, tile, count)
        row_total = t_ref[:, 0:128]
        if count == 2:
            row_total = jnp.concatenate([row_total, row_total], axis=1)
        mix_tan = product_mix + weight_tan - row_total * mix
        mix_acc[:, cols] = jnp.where(keep, mix, mix_acc[:, cols])
        tan_acc[:, cols] = jnp.where(keep, mix_tan, tan_acc[:, cols])

    def step(n, carry):
        late = (n >= 4).astype(jnp.int32)
        head, tile = 2 * n + late, n + late
        mask = in_head(head, tile, 1).astype(jnp.float32).astype(jnp.bfloat16)
        q = query(q_ref, tile, 1) * mask
        qt = query(qt_ref, tile, 1) * mask
        both = jnp.concatenate([jnp.concatenate([q, jnp.zeros_like(q)], 1), jnp.concatenate([qt, q], 1)], 0)
        scores = nt(both, jnp.concatenate([load(0, tile, 1), load(2, tile, 1)], 1))
        s_ref[...] = scores[:CELLS]
        t_ref[...] = scores[CELLS:]
        softmax(head)
        mixed = nn(w_ref[...], jnp.concatenate([load(1, tile, 1), load(3, tile, 1)], 1))
        finish(head, tile, 1, mixed[:CELLS, :128], mixed[CELLS:, :128], mixed[:CELLS, 128:])
        head, tile = 2 * n + 1 - late, n
        mask = in_head(head, tile, 2).astype(jnp.float32).astype(jnp.bfloat16)
        q = query(q_ref, tile, 2) * mask
        qt = query(qt_ref, tile, 2) * mask
        scores = nt(jnp.concatenate([q, qt], 0), load(0, tile, 2))
        s_ref[...] = scores[:CELLS]
        t_ref[...] = scores[CELLS:] + nt(q, load(2, tile, 2))
        softmax(head)
        mixed = nn(w_ref[...], load(1, tile, 2))
        finish(head, tile, 2, mixed[:CELLS], mixed[CELLS:], nn(w_ref[pl.ds(0, CELLS), :], load(3, tile, 2)))
        return carry

    def chunk_step(n, carry):
        for chunk in range(CHUNKS):

            @pl.when(n == chunk)
            def _(chunk=chunk):
                if chunk:
                    advance(chunk)
                if chunk < 2:
                    swaps[chunk].wait_recv()
                run(sides, 4, chunk, "recv")
                run(corners, 6, chunk, "recv")

        return lax.fori_loop(2 * n, 2 * n + 2, step, carry)

    lax.fori_loop(0, CHUNKS, chunk_step, 0)
    mix_ref[...] = mix_acc[...].astype(jnp.bfloat16).reshape(WIN, WIN, D)
    tan_ref[...] = tan_acc[...].astype(jnp.bfloat16).reshape(WIN, WIN, D)

    for chunk in range(CHUNKS):
        run(strips, 0, chunk, "sent")
        run(sides, 4, chunk, "sent")
        run(corners, 6, chunk, "sent")
        relay_in(chunk, "sent")
        relay_out(chunk, "sent")
    drained(zbuf.at[pl.ds(0, NZ - 1)], misc_send.at[0])
    drained(part(FAR, 6), misc_send.at[1])
    for n, span in enumerate(groups):
        drained(part(FAR, 24, *span), misc_send.at[2 + n])
        swaps[n].wait_send()
    drained(part(NEAR, 6), misc_send.at[4])


def pool_weights(pool_near, pool_far):
    cell = np.arange(CELLS)
    block = (cell // 64) * 4 + (cell % 16) // 4
    member = jnp.asarray(np.arange(16)[:, None] == block[None, :])
    near = jnp.where(member, jnp.tile(pool_near, (4, 4)).reshape(1, CELLS), 0.0)
    return jnp.concatenate([near, pool_far.reshape(1, CELLS), jnp.zeros((7, CELLS), jnp.float32)], axis=0)


def key_bias(level_bias):
    r, c = lax.axis_index("row"), lax.axis_index("col")
    group = np.arange(GROUPS)

    def within(first, count):
        return (group >= first) & (group < first + count)

    top = within(TOP, 16) | within(TL, 8) | within(TR, 8)
    bottom = within(BOTTOM, 16) | within(BL, 8) | within(BR, 8)
    left = within(LEFT, 16) | within(TL, 8) | within(BL, 8)
    right = within(RIGHT, 16) | within(TR, 8) | within(BR, 8)
    gone = (r == 0) & top | (r == 31) & bottom | (c == 0) & left | (c == 15) & right
    gone = gone | within(PAD, 8)
    bias = jnp.where(within(NEAR, 8), level_bias[0][:, None], jnp.where(within(FAR, 64), level_bias[1][:, None], 0.0))
    bias = jnp.where(gone[None, :], NEG, bias * LOG2E)
    return jnp.repeat(bias, 8, axis=1).reshape(HEADS, 1, KEYS)


def body(query_field, key_field, value_field, query_tan, key_tan, value_tan, pool_near, pool_far, level_bias):
    vmem = pl.BlockSpec(memory_space=pltpu.VMEM)
    anywhere = pl.BlockSpec(memory_space=pl.ANY)
    field = jax.ShapeDtypeStruct((WIN, WIN, D), jnp.bfloat16)
    stack, near, far = pl.pallas_call(
        prep_kernel,
        out_shape=(
            jax.ShapeDtypeStruct((4, WIN, WIN, D), jnp.bfloat16),
            jax.ShapeDtypeStruct((4, 16, D), jnp.bfloat16),
            jax.ShapeDtypeStruct((4, D), jnp.bfloat16),
        ),
        in_specs=[vmem] * 5,
        out_specs=(vmem, vmem, vmem),
        name="prep",
    )(pool_weights(pool_near, pool_far), key_field, value_field, key_tan, value_tan)
    halo = 10 * CHUNKS
    return pl.pallas_call(
        main_kernel,
        out_shape=(field, field),
        in_specs=[anywhere] * 5 + [vmem],
        out_specs=(vmem, vmem),
        scratch_shapes=[
            pltpu.VMEM((4, GROUPS, 8, D), jnp.bfloat16),
            pltpu.VMEM((NZ, 4, D), jnp.bfloat16),
            pltpu.VMEM((4, 8, 8, D), jnp.bfloat16),
            pltpu.VMEM((WIN, WIN, D), jnp.bfloat16),
            pltpu.VMEM((WIN, WIN, D), jnp.bfloat16),
            pltpu.VMEM((CELLS, KEYS), jnp.float32),
            pltpu.VMEM((CELLS, KEYS), jnp.float32),
            pltpu.VMEM((2 * CELLS, KEYS), jnp.bfloat16),
            pltpu.VMEM((CELLS, D), jnp.float32),
            pltpu.VMEM((CELLS, D), jnp.float32),
            pltpu.SemaphoreType.DMA((halo,)),
            pltpu.SemaphoreType.DMA((halo,)),
            pltpu.SemaphoreType.DMA((CHUNKS,)),
            pltpu.SemaphoreType.DMA((CHUNKS,)),
            pltpu.SemaphoreType.DMA((7,)),
            pltpu.SemaphoreType.DMA((7,)),
            pltpu.SemaphoreType.DMA((6,)),
        ],
        compiler_params=pltpu.CompilerParams(
            collective_id=0, has_side_effects=True, vmem_limit_bytes=60 * 1024 * 1024
        ),
        name="focal",
    )(
        stack.reshape(4, WIN, 2, 8, D), near.reshape(4, 2, 8, D), far, query_field, query_tan, key_bias(level_bias)
    )


def solution(mesh):
    spec = P("row", "col", None)
    return jax.shard_map(
        body, mesh=mesh, in_specs=(spec,) * 6 + (P(),) * 3, out_specs=(spec, spec), check_vma=False
    )
```

```python
import functools
import math

import jax
import jax.numpy as jnp
from jax import lax
from jax.experimental import pallas as pl
from jax.experimental.pallas import tpu as pltpu
from jax.sharding import PartitionSpec as P

HEADS = 16
HEAD_DIM = 72
D = 1152
WIN = 16
CELLS = WIN * WIN
NX, NY, NZ = 4, 4, 16
CHUNKS = D // 128
AHEAD = 2
MESH = pl.DeviceIdType.MESH
LOG2E = math.log2(math.e)
SCALE = HEAD_DIM**-0.5
NEG = -1e30

OWN, TOP, BOTTOM, LEFT, RIGHT = 0, 32, 48, 64, 80
TL, TR, BL, BR = 96, 104, 112, 120
NEAR, PAD, FAR = 128, 136, 144
GROUPS = 208
KEYS = GROUPS * 8
BLOCK = 32


def place():
    r, c = lax.axis_index("row"), lax.axis_index("col")
    y, x = r // 8, lax.rem(r, 4)
    z = lax.rem(r // 4, 2) * 8 + c // 2
    return r, c, x, y, z, lax.rem(c, 2)


def device(x, y, z, core):
    return (y * 8 + (z // 8) * 4 + x, lax.rem(z, 8) * 2 + core)


def main_kernel(
    k_in, v_in, kt_in, vt_in, q_in, qt_in, pool_near, pool_far, level_bias,
    mix_ref, tan_ref,
    keys, zbuf, relay, q_ref, qt_ref, s_ref, t_ref, w_ref, row_ref, sum_ref, mix_acc, tan_acc,
    halo_send, halo_recv, relay_send, relay_recv, misc_send, misc_recv, local_sem,
):
    r, c, x, y, z, core = place()
    fields = (k_in, v_in, kt_in, vt_in)
    up, down, west, east = r > 0, r < 31, c > 0, c < 15
    z_peers = [lax.rem(z + k, NZ) for k in range(1, NZ)]
    x_peers = [lax.rem(x + k, NX) for k in range(1, NX)]
    y_peers = [lax.rem(y + k, NY) for k in range(1, NY)]
    x_near = x + 1 - 2 * lax.rem(x, 2)
    near_peers = [device(x_near, y, z, core), device(x, y, z, 1 - core), device(x_near, y, z, 1 - core)]

    def lanes(chunk, count=1):
        return pl.ds(pl.multiple_of(chunk * 128, 128), count * 128)

    def part(first, count, chunk=None, width=1):
        return keys.at[:, pl.ds(first, count), :, slice(None) if chunk is None else lanes(chunk, width)]

    def drained(ref, sem):
        pltpu.make_async_copy(ref, ref, sem).wait()

    place_x = lax.rem(r, 4)
    far_down, far_up = down & (place_x == 3), up & (place_x == 0)
    hops = jnp.where(place_x >= 2, 2, -2)
    paired = (r + hops >= 0) & (r + hops < 32)
    relays_down, relays_up = paired & (place_x == 2), paired & (place_x == 1)

    def cut(rows, half, chunk):
        return [field.at[rows, half, :, lanes(chunk)] for field in fields]

    def strips(chunk):
        low = [cut(pl.ds(8, 8), half, chunk) for half in range(2)]
        high = [cut(pl.ds(0, 8), half, chunk) for half in range(2)]
        return [
            (down, low[0], TOP, 8, (r + 1, c), up),
            (up, high[0], BOTTOM, 8, (r - 1, c), down),
            (down & (place_x != 3), low[1], TOP + 8, 8, (r + 1, c), up),
            (up & (place_x != 0), high[1], BOTTOM + 8, 8, (r - 1, c), down),
        ]

    def relay_in(chunk, what):
        arrived = relay.at[:, :, :, lanes(chunk)]
        for n, cond, row, target in ((2, far_down, 8, (r - 1, c)), (3, far_up, 0, (r + 1, c))):
            slot = chunk * 10 + n

            @pl.when(cond)
            def _(row=row, target=target, slot=slot):
                if what == "start":
                    for f, src in enumerate(cut(pl.ds(row, 8), 1, chunk)):
                        pltpu.make_async_remote_copy(
                            src_ref=src, dst_ref=relay.at[f, :, :, lanes(chunk)],
                            send_sem=halo_send.at[slot], recv_sem=relay_recv.at[chunk],
                            device_id=target, device_id_type=MESH,
                        ).start()
                else:
                    drained(arrived, halo_send.at[slot])

    def relay_out(chunk, what):
        for n, cond, first, row in ((2, relays_down, TOP + 8, r + 2), (3, relays_up, BOTTOM + 8, r - 2)):
            copy = pltpu.make_async_remote_copy(
                src_ref=relay.at[:, :, :, lanes(chunk)], dst_ref=part(first, 8, chunk),
                send_sem=relay_send.at[chunk], recv_sem=halo_recv.at[chunk * 10 + n],
                device_id=(row, c), device_id_type=MESH,
            )
            if what == "start":
                arrived = relay.at[:, :, :, lanes(chunk)]

                @pl.when(cond)
                def _(copy=copy, arrived=arrived):
                    drained(arrived, relay_recv.at[chunk])
                    copy.start()
            else:
                pl.when(cond)(copy.wait_send)

    def sides(chunk):
        return [
            (east, cut(slice(None), 1, chunk), LEFT, 16, (r, c + 1), west),
            (west, cut(slice(None), 0, chunk), RIGHT, 16, (r, c - 1), east),
        ]

    def corners(chunk):
        return [
            (up & east, part(TOP + 8, 8, chunk), TL, 8, (r, c + 1), up & west),
            (up & west, part(TOP, 8, chunk), TR, 8, (r, c - 1), up & east),
            (down & east, part(BOTTOM + 8, 8, chunk), BL, 8, (r, c + 1), down & west),
            (down & west, part(BOTTOM, 8, chunk), BR, 8, (r, c - 1), down & east),
        ]

    def run(make, base, chunk, what):
        for n, (sends, src, first, count, target, receives) in enumerate(make(chunk)):
            slot = chunk * 10 + base + n
            whole = part(first, count, chunk)
            pairs = [(src, whole)]
            if isinstance(src, list):
                pairs = [(one, keys.at[f, pl.ds(first, count), :, lanes(chunk)]) for f, one in enumerate(src)]

            def go(pairs=pairs, slot=slot, target=target):
                for one, dst in pairs:
                    pltpu.make_async_remote_copy(
                        src_ref=one, dst_ref=dst, send_sem=halo_send.at[slot], recv_sem=halo_recv.at[slot],
                        device_id=target, device_id_type=MESH,
                    ).start()

            if what == "start":
                pl.when(sends)(go)
            elif what == "recv":
                pl.when(receives)(functools.partial(drained, whole, halo_recv.at[slot]))
            else:
                pl.when(sends)(functools.partial(drained, whole, halo_send.at[slot]))

    def to(src, dst, slot, target):
        return pltpu.make_async_remote_copy(
            src_ref=src, dst_ref=dst, send_sem=misc_send.at[slot], recv_sem=misc_recv.at[slot],
            device_id=target, device_id_type=MESH,
        )

    near_slot = NEAR + 2 * (lax.rem(x, 2) * 2 + core)
    for f, field in enumerate(fields):
        for half in range(2):
            pltpu.make_async_copy(field.at[:, half], keys.at[f, pl.ds(OWN + 16 * half, 16)], local_sem.at[0]).start()
    local = [pltpu.make_async_copy(q_in, q_ref, local_sem.at[1]), pltpu.make_async_copy(qt_in, qt_ref, local_sem.at[2])]
    for copy in local:
        copy.start()

    barrier = pltpu.get_barrier_semaphore()

    def greet(target):
        pl.semaphore_signal(barrier, inc=1, device_id=target, device_id_type=MESH)

    for cond, target in ((down, (r + 1, c)), (up, (r - 1, c)), (east, (r, c + 1)), (west, (r, c - 1))):
        pl.when(cond)(functools.partial(greet, target))
    fixed = (
        [device(x, y, p, core) for p in z_peers]
        + [device(p, y, z, core) for p in x_peers]
        + [device(x, p, z, core) for p in y_peers]
        + [device(x, y, z, 1 - core), device(x_near, y, z, 1 - core)]
    )
    for target in fixed:
        greet(target)
    pl.when(paired)(functools.partial(greet, (r + hops, c)))
    def clear(first, count):
        keys[:, pl.ds(first, count)] = jnp.zeros((4, count, 8, D), jnp.bfloat16)

    clear(PAD, FAR - PAD)
    for present, first, count in ((up, TOP, 16), (down, BOTTOM, 16), (west, LEFT, 16), (east, RIGHT, 16)):
        pl.when(jnp.logical_not(present))(functools.partial(clear, first, count))
    for present, first in ((up & west, TL), (up & east, TR), (down & west, BL), (down & east, BR)):
        pl.when(jnp.logical_not(present))(functools.partial(clear, first, 8))

    cell = lax.broadcasted_iota(jnp.int32, (16, CELLS), 1)
    row, col = (cell >> 3) & 15, (cell >> 7) * 8 + (cell & 7)
    in_block = lax.broadcasted_iota(jnp.int32, (16, CELLS), 0) == (row >> 2) * 4 + (col >> 2)
    weights = jnp.zeros((16, CELLS), jnp.float32)
    for p in range(4):
        for q in range(4):
            weights = jnp.where(in_block & ((row & 3) == p) & ((col & 3) == q), pool_near[p, q], weights)
    weights = jnp.concatenate([weights, jnp.broadcast_to(pool_far[...], (16, CELLS))], axis=0)
    high = weights.astype(jnp.bfloat16)
    rest = weights - high.astype(jnp.float32)
    middle = rest.astype(jnp.bfloat16)
    lowest = (rest - middle.astype(jnp.float32)).astype(jnp.bfloat16)
    drained(part(OWN, 32), local_sem.at[0])
    far_rows = []
    for f in range(4):
        flat = keys[f, pl.ds(OWN, 32)].reshape(CELLS, D)
        pooled = jnp.dot(lowest, flat, preferred_element_type=jnp.float32)
        pooled += jnp.dot(middle, flat, preferred_element_type=jnp.float32)
        pooled += jnp.dot(high, flat, preferred_element_type=jnp.float32)
        keys[f, pl.ds(near_slot, 2)] = pooled[:16].astype(jnp.bfloat16).reshape(2, 8, D)
        far_rows.append(pooled[16:17])
    zbuf[z] = jnp.concatenate(far_rows, axis=0).astype(jnp.bfloat16)
    edges = sum(cond.astype(jnp.int32) for cond in (down, up, east, west, paired))
    pl.semaphore_wait(barrier, len(fixed) + edges)

    def each(first, last, act):
        def body(chunk, carry):
            act(chunk)
            return carry

        lax.fori_loop(first, last, body, 0)

    def start(chunk):
        run(strips, 0, chunk, "start")
        run(sides, 4, chunk, "start")

    each(0, 1, lambda chunk: relay_in(chunk, "start"))
    for p in z_peers:
        to(zbuf.at[z], zbuf.at[z], 0, device(x, y, p, core)).start()

    def first_chunks(chunk):
        pl.when(chunk > 0)(lambda: relay_in(chunk, "start"))
        start(chunk)

    each(0, AHEAD, first_chunks)
    for target in near_peers:
        to(part(near_slot, 2), part(near_slot, 2), 4, target).start()

    far_group = FAR + 32 * core + 8 * y + 2 * x
    drained(zbuf.at[pl.ds(0, NZ - 1)], misc_recv.at[0])
    for f in range(4):
        cells = jnp.concatenate([zbuf[n].astype(jnp.float32)[f : f + 1] for n in range(NZ)], axis=0)
        keys[f, pl.ds(far_group, 2)] = cells.astype(jnp.bfloat16).reshape(2, 8, D)
    for copy in local:
        copy.wait()
    for p in x_peers:
        to(part(far_group, 2), part(far_group, 2), 1, device(p, y, z, core)).start()
    each(AHEAD, CHUNKS, lambda chunk: relay_in(chunk, "start"))
    each(0, AHEAD, lambda chunk: relay_out(chunk, "start"))
    drained(part(FAR, 6), misc_recv.at[1])
    far_y, far_core = FAR + 32 * core + 8 * y, FAR + 32 * core
    groups = ((0, 3), (3, CHUNKS - 3))

    def send_y(n):
        for p in y_peers:
            to(part(far_y, 8, *groups[n]), part(far_y, 8, *groups[n]), 2 + n, device(x, p, z, core)).start()

    swaps = [
        to(part(far_core, 32, *span), part(far_core, 32, *span), 5 + n, device(x, y, z, 1 - core))
        for n, span in enumerate(groups)
    ]
    send_y(0)
    drained(part(FAR, 24, *groups[0]), misc_recv.at[2])
    swaps[0].start()
    send_y(1)

    def advance(chunk):
        run(strips, 0, chunk, "recv")
        run(corners, 6, chunk, "start")

        @pl.when(chunk + AHEAD < CHUNKS)
        def _():
            start(chunk + AHEAD)
            relay_out(chunk + AHEAD, "start")

    def landed(chunk):
        run(sides, 4, chunk, "recv")
        run(corners, 6, chunk, "recv")

    each(0, 2, advance)
    drained(part(FAR, 24, *groups[1]), misc_recv.at[3])
    swaps[1].start()
    drained(part(NEAR, 6), misc_recv.at[4])

    def load(f, tile, count):
        width = 128 * count
        return keys[f, :, :, pl.ds(pl.multiple_of(tile * 128, 128), width)].reshape(KEYS, width)

    def query(ref, tile, count):
        width = 128 * count
        return ref[:, :, pl.ds(pl.multiple_of(tile * 128, 128), width)].reshape(CELLS, width)

    def in_head(head, tile, count):
        lane = lax.broadcasted_iota(jnp.int32, (1, 128 * count), 1) + tile * 128 - head * HEAD_DIM
        return (lane >= 0) & (lane < HEAD_DIM)

    def nt(a, b):
        return lax.dot_general(a, b, (((1,), (1,)), ((), ())), preferred_element_type=jnp.float32)

    def nn(a, b):
        return jnp.dot(a, b, preferred_element_type=jnp.float32)

    def tiles():
        return [slice(tile * 128, tile * 128 + 128) for tile in range(KEYS // 128)]

    def spread(column):
        return jnp.broadcast_to(column, (CELLS, 128))

    def gone(present):
        return jnp.where(present, 0.0, NEG).astype(jnp.float32)

    def put_scores(head, scores, tangent):
        near_bias, far_bias = level_bias[0, head] * LOG2E, level_bias[1, head] * LOG2E
        left_half = lax.broadcasted_iota(jnp.int32, (1, 128), 1) < 64
        offsets = [None, None, gone(up), gone(down), gone(west), gone(east)]
        offsets.append(jnp.where(left_half, gone(up & west), gone(up & east)))
        offsets.append(jnp.where(left_half, gone(down & west), gone(down & east)))
        offsets.append(jnp.where(left_half, near_bias, NEG))
        top = None
        for n, cols in enumerate(tiles()):
            scaled = scores[:, cols] * (SCALE * LOG2E)
            offset = offsets[n] if n < len(offsets) else far_bias
            scaled = scaled if offset is None else scaled + offset
            s_ref[:, cols] = scaled
            t_ref[:, cols] = tangent[:, cols] * SCALE
            top = scaled if top is None else jnp.maximum(top, scaled)
        row_ref[...] = spread(jnp.max(top, axis=1, keepdims=True))

    def softmax():
        def exponentials(n, carry):
            rows = pl.ds(pl.multiple_of(n * BLOCK, BLOCK), BLOCK)
            top = row_ref[rows, :]
            total = None
            for cols in tiles():
                expd = jnp.exp2(s_ref[rows, cols] - top)
                s_ref[rows, cols] = expd
                total = expd if total is None else total + expd
            sum_ref[rows, :] = total
            return carry

        def products(n, carry):
            rows = pl.ds(pl.multiple_of(n * BLOCK, BLOCK), BLOCK)
            late = pl.ds(pl.multiple_of(CELLS + n * BLOCK, BLOCK), BLOCK)
            inverse = row_ref[rows, :]
            total = None
            for cols in tiles():
                weights = s_ref[rows, cols] * inverse
                product = weights * t_ref[rows, cols]
                w_ref[rows, cols] = weights.astype(jnp.bfloat16)
                w_ref[late, cols] = product.astype(jnp.bfloat16)
                total = product if total is None else total + product
            sum_ref[rows, :] = total
            return carry

        lax.fori_loop(0, CELLS // BLOCK, exponentials, 0)
        row_ref[...] = spread(1.0 / jnp.sum(sum_ref[...], axis=1, keepdims=True))
        lax.fori_loop(0, CELLS // BLOCK, products, 0)

    def finish(head, tile, count, mix, product_mix, weight_tan):
        cols = pl.ds(pl.multiple_of(tile * 128, 128), 128 * count)
        keep = in_head(head, tile, count)
        row_total = jnp.sum(sum_ref[...], axis=1, keepdims=True)
        mix_tan = product_mix + weight_tan - row_total * mix
        mix_acc[:, cols] = jnp.where(keep, mix, mix_acc[:, cols])
        tan_acc[:, cols] = jnp.where(keep, mix_tan, tan_acc[:, cols])

    def step(n, carry):
        late = (n >= 4).astype(jnp.int32)
        head, tile = 2 * n + late, n + late
        mask = in_head(head, tile, 1).astype(jnp.float32).astype(jnp.bfloat16)
        q = query(q_ref, tile, 1) * mask
        qt = query(qt_ref, tile, 1) * mask
        both = jnp.concatenate([jnp.concatenate([q, jnp.zeros_like(q)], 1), jnp.concatenate([qt, q], 1)], 0)
        scores = nt(both, jnp.concatenate([load(0, tile, 1), load(2, tile, 1)], 1))
        put_scores(head, scores[:CELLS], scores[CELLS:])
        softmax()
        mixed = nn(w_ref[...], jnp.concatenate([load(1, tile, 1), load(3, tile, 1)], 1))
        finish(head, tile, 1, mixed[:CELLS, :128], mixed[CELLS:, :128], mixed[:CELLS, 128:])
        head, tile = 2 * n + 1 - late, n
        mask = in_head(head, tile, 2).astype(jnp.float32).astype(jnp.bfloat16)
        q = query(q_ref, tile, 2) * mask
        qt = query(qt_ref, tile, 2) * mask
        scores = nt(jnp.concatenate([q, qt], 0), load(0, tile, 2))
        put_scores(head, scores[:CELLS], scores[CELLS:] + nt(q, load(2, tile, 2)))
        softmax()
        mixed = nn(w_ref[...], load(1, tile, 2))
        finish(head, tile, 2, mixed[:CELLS], mixed[CELLS:], nn(w_ref[pl.ds(0, CELLS), :], load(3, tile, 2)))
        return carry

    swaps[0].wait_recv()
    landed(0)

    def chunk_step(n, carry):
        pl.when(n + 2 < CHUNKS)(lambda: advance(n + 2))
        pl.when(n == 2)(swaps[1].wait_recv)
        landed(n + 1)
        return step(n, carry)

    lax.fori_loop(0, HEADS // 2, chunk_step, 0)
    mix_ref[...] = mix_acc[...].astype(jnp.bfloat16).reshape(WIN, WIN, D)
    tan_ref[...] = tan_acc[...].astype(jnp.bfloat16).reshape(WIN, WIN, D)

    def sent(chunk):
        run(strips, 0, chunk, "sent")
        run(sides, 4, chunk, "sent")
        run(corners, 6, chunk, "sent")
        relay_in(chunk, "sent")
        relay_out(chunk, "sent")

    each(0, CHUNKS, sent)
    drained(zbuf.at[pl.ds(0, NZ - 1)], misc_send.at[0])
    drained(part(FAR, 6), misc_send.at[1])
    for n, span in enumerate(groups):
        drained(part(FAR, 24, *span), misc_send.at[2 + n])
        swaps[n].wait_send()
    drained(part(NEAR, 6), misc_send.at[4])


def body(query_field, key_field, value_field, query_tan, key_tan, value_tan, pool_near, pool_far, level_bias):
    vmem = pl.BlockSpec(memory_space=pltpu.VMEM)
    smem = pl.BlockSpec(memory_space=pltpu.SMEM)
    anywhere = pl.BlockSpec(memory_space=pl.ANY)
    field = jax.ShapeDtypeStruct((WIN, WIN, D), jnp.bfloat16)
    halo = 10 * CHUNKS
    return pl.pallas_call(
        main_kernel,
        out_shape=(field, field),
        in_specs=[anywhere] * 6 + [smem, vmem, smem],
        out_specs=(vmem, vmem),
        scratch_shapes=[
            pltpu.VMEM((4, GROUPS, 8, D), jnp.bfloat16),
            pltpu.VMEM((NZ, 4, D), jnp.bfloat16),
            pltpu.VMEM((4, 8, 8, D), jnp.bfloat16),
            pltpu.VMEM((WIN, WIN, D), jnp.bfloat16),
            pltpu.VMEM((WIN, WIN, D), jnp.bfloat16),
            pltpu.VMEM((CELLS, KEYS), jnp.float32),
            pltpu.VMEM((CELLS, KEYS), jnp.float32),
            pltpu.VMEM((2 * CELLS, KEYS), jnp.bfloat16),
            pltpu.VMEM((CELLS, 128), jnp.float32),
            pltpu.VMEM((CELLS, 128), jnp.float32),
            pltpu.VMEM((CELLS, D), jnp.float32),
            pltpu.VMEM((CELLS, D), jnp.float32),
            pltpu.SemaphoreType.DMA((halo,)),
            pltpu.SemaphoreType.DMA((halo,)),
            pltpu.SemaphoreType.DMA((CHUNKS,)),
            pltpu.SemaphoreType.DMA((CHUNKS,)),
            pltpu.SemaphoreType.DMA((7,)),
            pltpu.SemaphoreType.DMA((7,)),
            pltpu.SemaphoreType.DMA((3,)),
        ],
        compiler_params=pltpu.CompilerParams(
            collective_id=0, has_side_effects=True, vmem_limit_bytes=60 * 1024 * 1024
        ),
        name="focal",
    )(
        *(field.reshape(WIN, 2, 8, D) for field in (key_field, value_field, key_tan, value_tan)),
        query_field, query_tan, pool_near,
        pool_far.reshape(WIN, 2, 8).transpose(1, 0, 2).reshape(1, CELLS), level_bias,
    )


def solution(mesh):
    spec = P("row", "col", None)
    return jax.shard_map(
        body, mesh=mesh, in_specs=(spec,) * 6 + (P(),) * 3, out_specs=(spec, spec), check_vma=False
    )
```

```python
import functools
import math

import jax
import jax.numpy as jnp
from jax import lax
from jax.experimental import pallas as pl
from jax.experimental.pallas import tpu as pltpu
from jax.sharding import PartitionSpec as P

HEADS = 16
HEAD_DIM = 72
D = 1152
WIN = 16
CELLS = WIN * WIN
NX, NY, NZ = 4, 4, 16
CHUNKS = D // 128
AHEAD = 2
MESH = pl.DeviceIdType.MESH
LOG2E = math.log2(math.e)
SCALE = HEAD_DIM**-0.5
NEG = -1e30

OWN, TOP, BOTTOM, LEFT, RIGHT = 0, 32, 48, 64, 80
TL, TR, BL, BR = 96, 104, 112, 120
NEAR, PAD, FAR = 128, 136, 144
GROUPS = 208
KEYS = GROUPS * 8
BLOCK = 64


def place():
    r, c = lax.axis_index("row"), lax.axis_index("col")
    y, x = r // 8, lax.rem(r, 4)
    z = lax.rem(r // 4, 2) * 8 + c // 2
    return r, c, x, y, z, lax.rem(c, 2)


def device(x, y, z, core):
    return (y * 8 + (z // 8) * 4 + x, lax.rem(z, 8) * 2 + core)


def main_kernel(
    k_in, v_in, kt_in, vt_in, q_in, qt_in, pool_near, pool_far, level_bias,
    mix_ref, tan_ref,
    keys, zbuf, relay, q_ref, qt_ref, s_ref, t_ref, w_ref, row_ref, sum_ref, mix_acc, tan_acc,
    halo_send, halo_recv, relay_send, relay_recv, misc_send, misc_recv, local_sem,
):
    r, c, x, y, z, core = place()
    fields = (k_in, v_in, kt_in, vt_in)
    up, down, west, east = r > 0, r < 31, c > 0, c < 15
    z_peers = [lax.rem(z + k, NZ) for k in range(1, NZ)]
    x_peers = [lax.rem(x + k, NX) for k in range(1, NX)]
    y_peers = [lax.rem(y + k, NY) for k in range(1, NY)]
    x_near = x + 1 - 2 * lax.rem(x, 2)
    near_peers = [device(x_near, y, z, core), device(x, y, z, 1 - core), device(x_near, y, z, 1 - core)]

    def lanes(chunk, count=1):
        return pl.ds(pl.multiple_of(chunk * 128, 128), count * 128)

    def part(first, count, chunk=None, width=1):
        return keys.at[:, pl.ds(first, count), :, slice(None) if chunk is None else lanes(chunk, width)]

    def drained(ref, sem):
        pltpu.make_async_copy(ref, ref, sem).wait()

    place_x = lax.rem(r, 4)
    far_down, far_up = down & (place_x == 3), up & (place_x == 0)
    hops = jnp.where(place_x >= 2, 2, -2)
    paired = (r + hops >= 0) & (r + hops < 32)
    relays_down, relays_up = paired & (place_x == 2), paired & (place_x == 1)

    def cut(rows, half, chunk):
        return [field.at[rows, half, :, lanes(chunk)] for field in fields]

    def strips(chunk):
        low = [cut(pl.ds(8, 8), half, chunk) for half in range(2)]
        high = [cut(pl.ds(0, 8), half, chunk) for half in range(2)]
        return [
            (down, low[0], TOP, 8, (r + 1, c), up),
            (up, high[0], BOTTOM, 8, (r - 1, c), down),
            (down & (place_x != 3), low[1], TOP + 8, 8, (r + 1, c), up),
            (up & (place_x != 0), high[1], BOTTOM + 8, 8, (r - 1, c), down),
        ]

    def relay_in(chunk, what):
        arrived = relay.at[:, :, :, lanes(chunk)]
        for n, cond, row, target in ((2, far_down, 8, (r - 1, c)), (3, far_up, 0, (r + 1, c))):
            slot = chunk * 10 + n

            @pl.when(cond)
            def _(row=row, target=target, slot=slot):
                if what == "start":
                    for f, src in enumerate(cut(pl.ds(row, 8), 1, chunk)):
                        pltpu.make_async_remote_copy(
                            src_ref=src, dst_ref=relay.at[f, :, :, lanes(chunk)],
                            send_sem=halo_send.at[slot], recv_sem=relay_recv.at[chunk],
                            device_id=target, device_id_type=MESH,
                        ).start()
                else:
                    drained(arrived, halo_send.at[slot])

    def relay_out(chunk, what):
        for n, cond, first, row in ((2, relays_down, TOP + 8, r + 2), (3, relays_up, BOTTOM + 8, r - 2)):
            copy = pltpu.make_async_remote_copy(
                src_ref=relay.at[:, :, :, lanes(chunk)], dst_ref=part(first, 8, chunk),
                send_sem=relay_send.at[chunk], recv_sem=halo_recv.at[chunk * 10 + n],
                device_id=(row, c), device_id_type=MESH,
            )
            if what == "start":
                arrived = relay.at[:, :, :, lanes(chunk)]

                @pl.when(cond)
                def _(copy=copy, arrived=arrived):
                    drained(arrived, relay_recv.at[chunk])
                    copy.start()
            else:
                pl.when(cond)(copy.wait_send)

    def sides(chunk):
        return [
            (east, cut(slice(None), 1, chunk), LEFT, 16, (r, c + 1), west),
            (west, cut(slice(None), 0, chunk), RIGHT, 16, (r, c - 1), east),
        ]

    def corners(chunk):
        return [
            (up & east, part(TOP + 8, 8, chunk), TL, 8, (r, c + 1), up & west),
            (up & west, part(TOP, 8, chunk), TR, 8, (r, c - 1), up & east),
            (down & east, part(BOTTOM + 8, 8, chunk), BL, 8, (r, c + 1), down & west),
            (down & west, part(BOTTOM, 8, chunk), BR, 8, (r, c - 1), down & east),
        ]

    def run(make, base, chunk, what):
        for n, (sends, src, first, count, target, receives) in enumerate(make(chunk)):
            slot = chunk * 10 + base + n
            whole = part(first, count, chunk)
            pairs = [(src, whole)]
            if isinstance(src, list):
                pairs = [(one, keys.at[f, pl.ds(first, count), :, lanes(chunk)]) for f, one in enumerate(src)]

            def go(pairs=pairs, slot=slot, target=target):
                for one, dst in pairs:
                    pltpu.make_async_remote_copy(
                        src_ref=one, dst_ref=dst, send_sem=halo_send.at[slot], recv_sem=halo_recv.at[slot],
                        device_id=target, device_id_type=MESH,
                    ).start()

            if what == "start":
                pl.when(sends)(go)
            elif what == "recv":
                pl.when(receives)(functools.partial(drained, whole, halo_recv.at[slot]))
            else:
                pl.when(sends)(functools.partial(drained, whole, halo_send.at[slot]))

    def to(src, dst, slot, target):
        return pltpu.make_async_remote_copy(
            src_ref=src, dst_ref=dst, send_sem=misc_send.at[slot], recv_sem=misc_recv.at[slot],
            device_id=target, device_id_type=MESH,
        )

    near_slot = NEAR + 2 * (lax.rem(x, 2) * 2 + core)
    for f, field in enumerate(fields):
        for half in range(2):
            pltpu.make_async_copy(field.at[:, half], keys.at[f, pl.ds(OWN + 16 * half, 16)], local_sem.at[0]).start()
    local = [pltpu.make_async_copy(q_in, q_ref, local_sem.at[1]), pltpu.make_async_copy(qt_in, qt_ref, local_sem.at[2])]
    for copy in local:
        copy.start()

    barrier = pltpu.get_barrier_semaphore()

    def greet(target):
        pl.semaphore_signal(barrier, inc=1, device_id=target, device_id_type=MESH)

    for cond, target in ((down, (r + 1, c)), (up, (r - 1, c)), (east, (r, c + 1)), (west, (r, c - 1))):
        pl.when(cond)(functools.partial(greet, target))
    fixed = (
        [device(x, y, p, core) for p in z_peers]
        + [device(p, y, z, core) for p in x_peers]
        + [device(x, p, z, core) for p in y_peers]
        + [device(x, y, z, 1 - core), device(x_near, y, z, 1 - core)]
    )
    for target in fixed:
        greet(target)
    pl.when(paired)(functools.partial(greet, (r + hops, c)))
    def clear(first, count):
        keys[:, pl.ds(first, count)] = jnp.zeros((4, count, 8, D), jnp.bfloat16)

    clear(PAD, FAR - PAD)
    for present, first, count in ((up, TOP, 16), (down, BOTTOM, 16), (west, LEFT, 16), (east, RIGHT, 16)):
        pl.when(jnp.logical_not(present))(functools.partial(clear, first, count))
    for present, first in ((up & west, TL), (up & east, TR), (down & west, BL), (down & east, BR)):
        pl.when(jnp.logical_not(present))(functools.partial(clear, first, 8))

    cell = lax.broadcasted_iota(jnp.int32, (16, CELLS), 1)
    row, col = (cell >> 3) & 15, (cell >> 7) * 8 + (cell & 7)
    in_block = lax.broadcasted_iota(jnp.int32, (16, CELLS), 0) == (row >> 2) * 4 + (col >> 2)
    weights = jnp.zeros((16, CELLS), jnp.float32)
    for p in range(4):
        for q in range(4):
            weights = jnp.where(in_block & ((row & 3) == p) & ((col & 3) == q), pool_near[p, q], weights)
    weights = jnp.concatenate([weights, jnp.broadcast_to(pool_far[...], (16, CELLS))], axis=0)
    high = weights.astype(jnp.bfloat16)
    rest = weights - high.astype(jnp.float32)
    middle = rest.astype(jnp.bfloat16)
    lowest = (rest - middle.astype(jnp.float32)).astype(jnp.bfloat16)
    drained(part(OWN, 32), local_sem.at[0])
    far_rows = []
    for f in range(4):
        flat = keys[f, pl.ds(OWN, 32)].reshape(CELLS, D)
        pooled = jnp.dot(lowest, flat, preferred_element_type=jnp.float32)
        pooled += jnp.dot(middle, flat, preferred_element_type=jnp.float32)
        pooled += jnp.dot(high, flat, preferred_element_type=jnp.float32)
        keys[f, pl.ds(near_slot, 2)] = pooled[:16].astype(jnp.bfloat16).reshape(2, 8, D)
        far_rows.append(pooled[16:17])
    zbuf[z] = jnp.concatenate(far_rows, axis=0).astype(jnp.bfloat16)
    edges = sum(cond.astype(jnp.int32) for cond in (down, up, east, west, paired))
    pl.semaphore_wait(barrier, len(fixed) + edges)

    def each(first, last, act):
        def body(chunk, carry):
            act(chunk)
            return carry

        lax.fori_loop(first, last, body, 0)

    def start(chunk):
        run(strips, 0, chunk, "start")
        run(sides, 4, chunk, "start")

    each(0, 1, lambda chunk: relay_in(chunk, "start"))
    for p in z_peers:
        to(zbuf.at[z], zbuf.at[z], 0, device(x, y, p, core)).start()

    def first_chunks(chunk):
        pl.when(chunk > 0)(lambda: relay_in(chunk, "start"))
        start(chunk)

    each(0, AHEAD, first_chunks)
    for target in near_peers:
        to(part(near_slot, 2), part(near_slot, 2), 4, target).start()

    far_group = FAR + 32 * core + 8 * y + 2 * x
    drained(zbuf.at[pl.ds(0, NZ - 1)], misc_recv.at[0])
    for f in range(4):
        cells = jnp.concatenate([zbuf[n].astype(jnp.float32)[f : f + 1] for n in range(NZ)], axis=0)
        keys[f, pl.ds(far_group, 2)] = cells.astype(jnp.bfloat16).reshape(2, 8, D)
    for copy in local:
        copy.wait()
    for p in x_peers:
        to(part(far_group, 2), part(far_group, 2), 1, device(p, y, z, core)).start()
    each(AHEAD, CHUNKS, lambda chunk: relay_in(chunk, "start"))
    each(0, AHEAD, lambda chunk: relay_out(chunk, "start"))
    drained(part(FAR, 6), misc_recv.at[1])
    far_y, far_core = FAR + 32 * core + 8 * y, FAR + 32 * core
    groups = ((0, 3), (3, CHUNKS - 3))

    def send_y(n):
        for p in y_peers:
            to(part(far_y, 8, *groups[n]), part(far_y, 8, *groups[n]), 2 + n, device(x, p, z, core)).start()

    swaps = [
        to(part(far_core, 32, *span), part(far_core, 32, *span), 5 + n, device(x, y, z, 1 - core))
        for n, span in enumerate(groups)
    ]
    send_y(0)
    def advance(chunk):
        run(strips, 0, chunk, "recv")
        run(corners, 6, chunk, "start")

        @pl.when(chunk + AHEAD < CHUNKS)
        def _():
            start(chunk + AHEAD)
            relay_out(chunk + AHEAD, "start")

    def landed(chunk):
        run(sides, 4, chunk, "recv")
        run(corners, 6, chunk, "recv")

    each(0, 1, advance)
    drained(part(FAR, 24, *groups[0]), misc_recv.at[2])
    swaps[0].start()
    send_y(1)

    each(1, 2, advance)
    drained(part(FAR, 24, *groups[1]), misc_recv.at[3])
    swaps[1].start()
    drained(part(NEAR, 6), misc_recv.at[4])

    def load(f, tile, count):
        width = 128 * count
        return keys[f, :, :, pl.ds(pl.multiple_of(tile * 128, 128), width)].reshape(KEYS, width)

    def query(ref, tile, count):
        width = 128 * count
        return ref[:, :, pl.ds(pl.multiple_of(tile * 128, 128), width)].reshape(CELLS, width)

    def in_head(head, tile, count):
        lane = lax.broadcasted_iota(jnp.int32, (1, 128 * count), 1) + tile * 128 - head * HEAD_DIM
        return (lane >= 0) & (lane < HEAD_DIM)

    def nt(a, b):
        return lax.dot_general(a, b, (((1,), (1,)), ((), ())), preferred_element_type=jnp.float32)

    def nn(a, b):
        return jnp.dot(a, b, preferred_element_type=jnp.float32)

    def tiles():
        return [slice(tile * 128, tile * 128 + 128) for tile in range(KEYS // 128)]

    def spread(column):
        return jnp.broadcast_to(column, (CELLS, 128))

    def gone(present):
        return jnp.where(present, 0.0, NEG).astype(jnp.float32)

    def put_scores(head, scores, tangent):
        near_bias, far_bias = level_bias[0, head] * LOG2E, level_bias[1, head] * LOG2E
        left_half = lax.broadcasted_iota(jnp.int32, (1, 128), 1) < 64
        offsets = [None, None, gone(up), gone(down), gone(west), gone(east)]
        offsets.append(jnp.where(left_half, gone(up & west), gone(up & east)))
        offsets.append(jnp.where(left_half, gone(down & west), gone(down & east)))
        offsets.append(jnp.where(left_half, near_bias, NEG))
        top = None
        for n, cols in enumerate(tiles()):
            scaled = scores[:, cols] * (SCALE * LOG2E)
            offset = offsets[n] if n < len(offsets) else far_bias
            scaled = scaled if offset is None else scaled + offset
            s_ref[:, cols] = scaled
            t_ref[:, cols] = tangent[:, cols] * SCALE
            top = scaled if top is None else jnp.maximum(top, scaled)
        row_ref[...] = spread(jnp.max(top, axis=1, keepdims=True))

    def softmax():
        def exponentials(n, carry):
            rows = pl.ds(pl.multiple_of(n * BLOCK, BLOCK), BLOCK)
            top = row_ref[rows, :]
            total = None
            for cols in tiles():
                expd = jnp.exp2(s_ref[rows, cols] - top)
                s_ref[rows, cols] = expd
                total = expd if total is None else total + expd
            sum_ref[rows, :] = total
            return carry

        def products(n, carry):
            rows = pl.ds(pl.multiple_of(n * BLOCK, BLOCK), BLOCK)
            late = pl.ds(pl.multiple_of(CELLS + n * BLOCK, BLOCK), BLOCK)
            inverse = row_ref[rows, :]
            total = None
            for cols in tiles():
                weights = s_ref[rows, cols] * inverse
                product = weights * t_ref[rows, cols]
                w_ref[rows, cols] = weights.astype(jnp.bfloat16)
                w_ref[late, cols] = product.astype(jnp.bfloat16)
                total = product if total is None else total + product
            sum_ref[rows, :] = total
            return carry

        lax.fori_loop(0, CELLS // BLOCK, exponentials, 0)
        row_ref[...] = spread(1.0 / jnp.sum(sum_ref[...], axis=1, keepdims=True))
        lax.fori_loop(0, CELLS // BLOCK, products, 0)

    def finish(head, tile, count, mix, product_mix, weight_tan):
        cols = pl.ds(pl.multiple_of(tile * 128, 128), 128 * count)
        keep = in_head(head, tile, count)
        row_total = jnp.sum(sum_ref[...], axis=1, keepdims=True)
        mix_tan = product_mix + weight_tan - row_total * mix
        mix_acc[:, cols] = jnp.where(keep, mix, mix_acc[:, cols])
        tan_acc[:, cols] = jnp.where(keep, mix_tan, tan_acc[:, cols])

    def step(n, carry):
        late = (n >= 4).astype(jnp.int32)
        head, tile = 2 * n + late, n + late
        mask = in_head(head, tile, 1).astype(jnp.float32).astype(jnp.bfloat16)
        q = query(q_ref, tile, 1) * mask
        qt = query(qt_ref, tile, 1) * mask
        both = jnp.concatenate([jnp.concatenate([q, jnp.zeros_like(q)], 1), jnp.concatenate([qt, q], 1)], 0)
        scores = nt(both, jnp.concatenate([load(0, tile, 1), load(2, tile, 1)], 1))
        put_scores(head, scores[:CELLS], scores[CELLS:])
        softmax()
        mixed = nn(w_ref[...], jnp.concatenate([load(1, tile, 1), load(3, tile, 1)], 1))
        finish(head, tile, 1, mixed[:CELLS, :128], mixed[CELLS:, :128], mixed[:CELLS, 128:])
        head, tile = 2 * n + 1 - late, n
        mask = in_head(head, tile, 2).astype(jnp.float32).astype(jnp.bfloat16)
        q = query(q_ref, tile, 2) * mask
        qt = query(qt_ref, tile, 2) * mask
        scores = nt(jnp.concatenate([q, qt], 0), load(0, tile, 2))
        put_scores(head, scores[:CELLS], scores[CELLS:] + nt(q, load(2, tile, 2)))
        softmax()
        mixed = nn(w_ref[...], load(1, tile, 2))
        finish(head, tile, 2, mixed[:CELLS], mixed[CELLS:], nn(w_ref[pl.ds(0, CELLS), :], load(3, tile, 2)))
        return carry

    swaps[0].wait_recv()
    landed(0)

    def chunk_step(n, carry):
        pl.when(n + 2 < CHUNKS)(lambda: advance(n + 2))
        pl.when(n == 2)(swaps[1].wait_recv)
        landed(n + 1)
        return step(n, carry)

    lax.fori_loop(0, HEADS // 2, chunk_step, 0)
    mix_ref[...] = mix_acc[...].astype(jnp.bfloat16).reshape(WIN, WIN, D)
    tan_ref[...] = tan_acc[...].astype(jnp.bfloat16).reshape(WIN, WIN, D)

    def sent(chunk):
        run(strips, 0, chunk, "sent")
        run(sides, 4, chunk, "sent")
        run(corners, 6, chunk, "sent")
        relay_in(chunk, "sent")
        relay_out(chunk, "sent")

    each(0, CHUNKS, sent)
    drained(zbuf.at[pl.ds(0, NZ - 1)], misc_send.at[0])
    drained(part(FAR, 6), misc_send.at[1])
    for n, span in enumerate(groups):
        drained(part(FAR, 24, *span), misc_send.at[2 + n])
        swaps[n].wait_send()
    drained(part(NEAR, 6), misc_send.at[4])


def body(query_field, key_field, value_field, query_tan, key_tan, value_tan, pool_near, pool_far, level_bias):
    vmem = pl.BlockSpec(memory_space=pltpu.VMEM)
    smem = pl.BlockSpec(memory_space=pltpu.SMEM)
    anywhere = pl.BlockSpec(memory_space=pl.ANY)
    field = jax.ShapeDtypeStruct((WIN, WIN, D), jnp.bfloat16)
    halo = 10 * CHUNKS
    return pl.pallas_call(
        main_kernel,
        out_shape=(field, field),
        in_specs=[anywhere] * 6 + [smem, vmem, smem],
        out_specs=(vmem, vmem),
        scratch_shapes=[
            pltpu.VMEM((4, GROUPS, 8, D), jnp.bfloat16),
            pltpu.VMEM((NZ, 4, D), jnp.bfloat16),
            pltpu.VMEM((4, 8, 8, D), jnp.bfloat16),
            pltpu.VMEM((WIN, WIN, D), jnp.bfloat16),
            pltpu.VMEM((WIN, WIN, D), jnp.bfloat16),
            pltpu.VMEM((CELLS, KEYS), jnp.float32),
            pltpu.VMEM((CELLS, KEYS), jnp.float32),
            pltpu.VMEM((2 * CELLS, KEYS), jnp.bfloat16),
            pltpu.VMEM((CELLS, 128), jnp.float32),
            pltpu.VMEM((CELLS, 128), jnp.float32),
            pltpu.VMEM((CELLS, D), jnp.float32),
            pltpu.VMEM((CELLS, D), jnp.float32),
            pltpu.SemaphoreType.DMA((halo,)),
            pltpu.SemaphoreType.DMA((halo,)),
            pltpu.SemaphoreType.DMA((CHUNKS,)),
            pltpu.SemaphoreType.DMA((CHUNKS,)),
            pltpu.SemaphoreType.DMA((7,)),
            pltpu.SemaphoreType.DMA((7,)),
            pltpu.SemaphoreType.DMA((3,)),
        ],
        compiler_params=pltpu.CompilerParams(
            collective_id=0, has_side_effects=True, vmem_limit_bytes=60 * 1024 * 1024
        ),
        name="focal",
    )(
        *(field.reshape(WIN, 2, 8, D) for field in (key_field, value_field, key_tan, value_tan)),
        query_field, query_tan, pool_near,
        pool_far.reshape(WIN, 2, 8).transpose(1, 0, 2).reshape(1, CELLS), level_bias,
    )


def solution(mesh):
    spec = P("row", "col", None)
    return jax.shard_map(
        body, mesh=mesh, in_specs=(spec,) * 6 + (P(),) * 3, out_specs=(spec, spec), check_vma=False
    )
```
